32 devices in a mesh: tm: 4 (over y, core), expert: 8 (over z, x).
Axes of the slice: x: 2, y: 2, z: 4, core: 2. Of those that a mesh axis runs over, the one named last changes fastest.
Arguments:
- states: bfloat16 [4, 1024, 2048], P('tm', 'expert'), may hold values from -6 to 6
- terminal: float32 [1024, 2048], P('expert'), may hold values from -6 to 6
- gates: float32 [4, 1024, 2], P('tm', 'expert'), may hold values from 0.25 to 1
- routes: int32 [4, 1024, 2], P('tm', 'expert'), may hold values from 0 to 7, all different within a row; in each aligned block of 32 rows (0 to 31, 32 to 63, ..., all dimensions but the last counted through in order) at most 12 rows name the same one
- w_in: bfloat16 [8, 2048, 2048], P('expert'), may hold values from -0.125 to 0.125
- w_out: bfloat16 [8, 2048, 2048], P('expert'), may hold values from -0.125 to 0.125
Outputs:
- adjoints: float32 [4, 1024, 2048], P('tm', 'expert')
The draws below stay inside these ranges and needn't reach their ends.
Inputs may be any that keep to these rules, and one draw needn't show every extreme that they name: `routes`: the 2 experts of a token at a step differ. In each aligned block of 32 rows of one step (one micro-batch of one device), no expert is named by more than 12 rows, a bound that some block reaches.
All inputs are finite; a program needn't handle non-finite values.
Results may differ from the reference program's by a relative error of at most 0.006.
Values may be sent and summed in bfloat16 or wider, within the bound.
A program may use at most 64 MiB of HBM per device.

```python
import math
import jax
import jax.numpy as jnp
import numpy as np
from jax import lax

D = 2048
FF = 2048
TOP = 2
MB = 32
TOKENS = 1024
EXPERTS = 8
NSTEP = 4
CAP = 12


def shard_levels(rng, extent, split, least, top_value):
    def one(axis_at, shards_of):
        heights = jax.random.uniform(jax.random.fold_in(jax.random.fold_in(rng, 6), axis_at), (shards_of,), jnp.float32, least / len(split), top_value / len(split))
        return jnp.repeat(jnp.exp(heights), extent[axis_at] // shards_of).reshape((-1,) + (1,) * (len(extent) - axis_at - 1))

    loudness = one(*split[0])
    for cut in split[1:]:
        loudness = loudness * one(*cut)
    return loudness


def deal_out(own_key, own, number, rows, count, top, reach, skew):
    ranking = jax.random.permutation(own_key, count)
    heavy_load, ordinary = load_shares(count, rows * top, reach, skew, True), load_shares(count, rows * top, reach, skew, False)
    places = jnp.arange(count)

    def named(sizes, turn):
        used = int((sizes > 0).sum())
        fixed = max(1, used // 4)
        passed = fixed + (places - fixed + turn * (used - fixed)) % max(1, count - fixed)
        return jnp.zeros((count,), jnp.int32).at[ranking[jnp.where(places < fixed, places, passed)]].set(jnp.asarray(sizes, jnp.int32))

    sizes = jnp.where(number % 4 == 0, named(heavy_load, number // 4), named(ordinary, number - number // 4 - 1))
    mixed = jax.random.permutation(jax.random.fold_in(own, 3), count)
    source_of, receiver = mixed[0:count // 2 * 2:2], mixed[1:count // 2 * 2:2]
    slack = jnp.minimum(sizes[source_of] - 1, reach - sizes[receiver]) // 2
    slack = jnp.where((source_of == ranking[0]) | (receiver == ranking[0]) | (sizes[receiver] == 0), 0, jnp.maximum(slack, 0))
    passed = jax.random.randint(jax.random.fold_in(own, 4), (count // 2,), 0, 1 << 20) % (slack + 1)
    sizes = sizes.at[source_of].add(-passed).at[receiver].add(passed)
    members = jnp.searchsorted(jnp.cumsum(sizes), jnp.arange(rows * top), side="right").astype(jnp.int32)
    table = members.reshape(top, rows).T
    table = table[jax.random.permutation(jax.random.fold_in(own, 1), rows)]
    turn = jax.random.randint(jax.random.fold_in(own, 2), (rows, 1), 0, top)
    return jnp.take_along_axis(table, (jnp.arange(top)[None, :] + turn) % top, axis=1)


def load_shares(count, total, reach, lean, full):
    loads = [(1 << 20) // math.isqrt(rank ** lean) + 1 for rank in range(1, count + 1)]
    largest = reach if full else min(reach, max(-(-total // count), total * loads[0] // sum(loads)))
    least = 1 if total - largest >= count - 1 else 0
    counts, rest = [largest] + [least] * (count - 1), total - largest - least * (count - 1)
    while rest > 0:
        free = [i for i in range(1, count) if counts[i] < largest] or [i for i in range(1, count) if counts[i] < reach]
        whole, remaining = sum([loads[i] for i in free]), rest
        for i in free:
            more = min(reach - counts[i], max(1, remaining * loads[i] // whole), rest)
            counts[i] = counts[i] + more
            rest = rest - more
    return np.array(counts)


def scatter_about(key, extent, deviation, most, pieces=(), kind=jnp.bfloat16):
    array = jax.random.normal(key, extent, jnp.float32) * deviation
    if len(pieces) > 0:
        array = shard_levels(key, extent, pieces, -0.22, 0.18) * array
    return jnp.clip(array, min=-most, max=most).astype(kind)


def setup_inputs(seed: int = 0) -> dict:
    arg_keys = jax.random.split(jax.random.key(seed), 7)
    states = scatter_about(arg_keys[0], (NSTEP, TOKENS, D), 1.0, 6.0, ((0, 4), (1, 8)))
    terminal = scatter_about(arg_keys[1], (TOKENS, D), 1.0, 6.0, ((0, 8),), jnp.float32)
    gates = jnp.clip(0.25 + 0.75 * jax.random.uniform(arg_keys[2], (NSTEP, TOKENS, TOP), jnp.float32) ** shard_levels(arg_keys[2], (NSTEP, TOKENS, TOP), ((0, 4), (1, 8)), -0.2, 0.2), 0.25, 1.0)
    routes_keys = jax.random.split(jax.random.fold_in(arg_keys[3], 1), NSTEP * TOKENS // MB)
    routes_turns = jax.random.permutation(jax.random.fold_in(arg_keys[3], 3), NSTEP * TOKENS // MB)
    routes = jax.vmap(lambda own, number: deal_out(jax.random.fold_in(arg_keys[3], 2), own, number, MB, EXPERTS, TOP, CAP, 2))(routes_keys, routes_turns).reshape((NSTEP, TOKENS, TOP))
    w_in = scatter_about(arg_keys[4], (EXPERTS, D, FF), D ** -0.5, 0.125, ((0, 8),))
    w_out = scatter_about(arg_keys[5], (EXPERTS, FF, D), FF ** -0.5, 0.125, ((0, 8),))
    return dict(states=states, terminal=terminal, gates=gates, routes=routes, w_in=w_in, w_out=w_out)


step_size = 0.5


def gelu_slope(preact):
    inside = 0.7978845608 * (preact + 0.044715 * preact ** 3)
    tangent = jnp.tanh(inside)
    return 0.5 * (1.0 + tangent) + 0.5 * preact * (1.0 - tangent * tangent) * 0.7978845608 * (1.0 + 3.0 * 0.044715 * preact * preact)


def reference(states, terminal, gates, routes, w_in, w_out):
    expert_count = w_in.shape[0]
    tokens = states.shape[1]
    width = states.shape[2]
    blocks = tokens // MB
    token_ids = jnp.arange(tokens, dtype=jnp.int32)
    owner_ids = jnp.repeat(token_ids, TOP)

    def one_step(adjoint, inputs):
        layer_in, step_gates, step_routes = inputs
        flattened = step_routes.reshape(blocks, MB * TOP)
        onehot = (flattened[:, :, None] == jnp.arange(expert_count, dtype=jnp.int32)[None, None, :]).astype(jnp.int32)
        running = jnp.cumsum(onehot, axis=1)
        slot = jnp.sum(onehot * running, axis=2) - 1
        target = (slot + (jnp.arange(blocks, dtype=jnp.int32) * CAP)[:, None]).reshape(-1).astype(jnp.int32)
        expert_flat = flattened.reshape(-1).astype(jnp.int32)
        slot_owner = jnp.full((expert_count, blocks * CAP), tokens, jnp.int32).at[expert_flat, target].set(owner_ids)
        rows_pad = jnp.concatenate([layer_in, jnp.zeros((1, width), jnp.bfloat16)], axis=0)
        adj_pad = jnp.concatenate([adjoint.astype(jnp.bfloat16), jnp.zeros((1, width), jnp.bfloat16)], axis=0)

        def per_expert(packed):
            row_index, weight_in, weight_out = packed
            state_rows = rows_pad[row_index]
            adjoint_rows = adj_pad[row_index]
            preact = jnp.dot(state_rows, weight_in, preferred_element_type=jnp.float32)
            back = lax.dot_general(adjoint_rows, weight_out, (((1,), (1,)), ((), ())), preferred_element_type=jnp.float32)
            hidden = (back * gelu_slope(preact)).astype(jnp.bfloat16)
            return lax.dot_general(hidden, weight_in, (((1,), (1,)), ((), ())), preferred_element_type=jnp.float32).astype(jnp.bfloat16)

        results = lax.map(per_expert, (slot_owner, w_in, w_out))
        picked = results[expert_flat, target].reshape(tokens, TOP, width).astype(jnp.float32)
        combined = jnp.sum(step_gates[:, :, None] * picked, axis=1)
        updated = adjoint + step_size * combined
        return updated, updated

    _, outputs = lax.scan(one_step, terminal, (states, gates, routes), reverse=True)
    return outputs
```

```python
import functools

import jax
import jax.numpy as jnp
from jax import lax
from jax.experimental import pallas as pl
from jax.experimental.pallas import tpu as pltpu
from jax.sharding import PartitionSpec as P

MB = 32
CHUNKS = 4
STEP_SIZE = 0.5
PAD = 16


def gelu_slope(v):
    inside = 0.7978845608 * (v + 0.044715 * (v * v * v))
    t = jnp.tanh(inside)
    return 0.5 * (1.0 + t) + 0.5 * v * (1.0 - t * t) * 0.7978845608 * (
        1.0 + 3.0 * 0.044715 * v * v
    )


def kernel(
    steps, experts, cap, rows,
    states, terminal, rg, w_in, w_out,
    out,
    win, wout, adj, sts, rgb, pmat, cmat, send_s, recv_s, send_a, recv_a, send_b, recv_b,
    slopes, back, hidden, collect,
    w_sem, loc_sem, rg_ssem, rg_rsem, st_ssem, st_rsem,
    s_ssem, s_rsem, a_ssem, a_rsem, b_ssem, b_rsem, o_ssem, o_rsem,
):
    t = lax.axis_index("tm")
    me = lax.axis_index("expert")
    width = win.shape[0]
    ff = win.shape[1]
    dc = width // CHUNKS
    fc = ff // CHUNKS
    slots = experts * PAD

    def cols(c):
        return pl.ds(c * dc, dc)

    def slab(e):
        return pl.ds(pl.multiple_of(e * PAD, PAD), PAD)

    def peer(k):
        return lax.rem(me + k, experts)

    def tm_peer(k):
        return lax.rem(t + k, steps)

    def remote(src, dst, ssem, rsem, axis, dev):
        return pltpu.make_async_remote_copy(
            src_ref=src, dst_ref=dst, send_sem=ssem, recv_sem=rsem,
            device_id={axis: dev}, device_id_type=pl.DeviceIdType.MESH,
        )

    def block_rows(b):
        return pl.ds(pl.multiple_of(b * rows, rows), rows)

    def w_copies():
        found = []
        for c in range(CHUNKS):
            part = pl.ds(c * fc, fc)
            found.append(pltpu.make_async_copy(w_in.at[0, :, part], win.at[:, part], w_sem.at[0, c]))
        for c in range(CHUNKS):
            found.append(
                pltpu.make_async_copy(w_out.at[0, :, cols(c)], wout.at[:, cols(c)], w_sem.at[1, c])
            )
        return found

    own_terminal = pltpu.make_async_copy(terminal.at[block_rows(t)], adj, loc_sem.at[0])
    own_terminal.start()
    own_states = pltpu.make_async_copy(states.at[0, block_rows(t)], sts.at[t], loc_sem.at[1])
    own_states.start()
    own_rg = pltpu.make_async_copy(rg.at[block_rows(t)], rgb.at[t], loc_sem.at[2])
    own_rg.start()
    weights = w_copies()
    for copy in weights:
        copy.start()

    zeros = jnp.zeros((slots, width), jnp.bfloat16)
    recv_a[...] = zeros
    recv_b[...] = zeros
    for s in range(steps):
        recv_s[s] = zeros

    barrier = pltpu.get_barrier_semaphore()
    for k in range(1, experts):
        pl.semaphore_signal(
            barrier, inc=1, device_id={"expert": peer(k)}, device_id_type=pl.DeviceIdType.MESH
        )
    for k in range(1, steps):
        pl.semaphore_signal(
            barrier, inc=1, device_id={"tm": tm_peer(k)}, device_id_type=pl.DeviceIdType.MESH
        )
    pl.semaphore_wait(barrier, experts + steps - 2)

    def rg_copy(k):
        b = tm_peer(k)
        return remote(rg.at[block_rows(b)], rgb.at[t], rg_ssem.at[k - 1], rg_rsem.at[k - 1], "tm", b)

    def st_copy(k):
        b = tm_peer(k)
        return remote(
            states.at[0, block_rows(b)], sts.at[t], st_ssem.at[k - 1], st_rsem.at[k - 1], "tm", b
        )

    for k in range(1, steps):
        rg_copy(k).start()
    for k in range(1, steps):
        st_copy(k).start()

    own_rg.wait()
    for k in range(1, steps):
        rg_copy(k).wait()

    lane = lax.broadcasted_iota(jnp.int32, (rows, slots), 1)
    lane_expert = (lane // PAD).astype(jnp.float32)
    lane_slot = (lane % PAD).astype(jnp.float32)
    earlier = (
        lax.broadcasted_iota(jnp.int32, (rows, rows), 1)
        < lax.broadcasted_iota(jnp.int32, (rows, rows), 0)
    ).astype(jnp.float32).astype(jnp.bfloat16)
    for s in range(steps):
        r0, r1 = rgb[s, :, 0:1], rgb[s, :, 1:2]
        g0, g1 = rgb[s, :, 2:3], rgb[s, :, 3:4]
        first = jnp.where(r0 == lane_expert, 1.0, 0.0)
        second = jnp.where(r1 == lane_expert, 1.0, 0.0)
        routed = first + second
        before = jnp.dot(earlier, routed.astype(jnp.bfloat16), preferred_element_type=jnp.float32)
        here = jnp.where(before == lane_slot, 1.0, 0.0)
        sel = routed * here
        pmat[s] = sel.T.astype(jnp.bfloat16)
        weight = STEP_SIZE * (g0 * first + g1 * second) * here
        high = weight.astype(jnp.bfloat16)
        cmat[s, 0:rows, :] = high
        cmat[s, rows:, :] = (weight - high.astype(jnp.float32)).astype(jnp.bfloat16)

    def a_copy(c, k):
        d = peer(k)
        return remote(
            send_a.at[slab(d), cols(c)], recv_a.at[slab(me), cols(c)],
            a_ssem.at[c, k - 1], a_rsem.at[c, k - 1], "expert", d,
        )

    def b_copy(c, k):
        d = peer(k)
        return remote(
            send_b.at[slab(d), cols(c)], recv_b.at[slab(me), cols(c)],
            b_ssem.at[c, k - 1], b_rsem.at[c, k - 1], "expert", d,
        )

    def s_copy(s, k):
        d = peer(k)
        return remote(
            send_s.at[s, slab(d)], recv_s.at[s, slab(me)],
            s_ssem.at[s, k - 1], s_rsem.at[s, k - 1], "expert", d,
        )

    own = pl.ds(pl.multiple_of(me * PAD, PAD), PAD)

    def pack_a(step, c):
        packed = jnp.dot(
            pmat[step], adj[:, cols(c)].astype(jnp.bfloat16), preferred_element_type=jnp.float32
        ).astype(jnp.bfloat16)
        send_a[:, cols(c)] = packed
        for k in range(1, experts):
            a_copy(c, k).start()
        recv_a[own, cols(c)] = send_a[own, cols(c)]

    def pack_s(s):
        for c in range(CHUNKS):
            send_s[s, :, cols(c)] = jnp.dot(
                pmat[s], sts[s, :, cols(c)], preferred_element_type=jnp.float32
            ).astype(jnp.bfloat16)
        for k in range(1, experts):
            s_copy(s, k).start()
        recv_s[s, own, :] = send_s[s, own, :]

    own_states.wait()
    for k in range(1, steps):
        st_copy(k).wait()
    pack_s(steps - 1)
    own_terminal.wait()
    for c in range(CHUNKS):
        pack_a(steps - 1, c)

    for copy in weights[:CHUNKS]:
        copy.wait()

    def make_slopes(s):
        for k in range(1, experts):
            s_copy(s, k).wait()
        rows_in = recv_s[s]
        for c in range(CHUNKS):
            part = pl.ds(c * fc, fc)
            pre = jnp.dot(rows_in, win[:, part], preferred_element_type=jnp.float32)
            slopes[:, part] = gelu_slope(pre)

    make_slopes(steps - 1)
    for copy in weights[CHUNKS:]:
        copy.wait()

    nt = (((1,), (1,)), ((), ()))

    def out_remote(s):
        return remote(
            collect.at[s], out.at[0, block_rows(t)], o_ssem.at[s], o_rsem.at[t], "tm", s
        )

    def out_local(s):
        return pltpu.make_async_copy(collect.at[s], out.at[0, block_rows(t)], loc_sem.at[3])

    def one_round(turn, carry):
        s = steps - 1 - turn
        more = turn < steps - 1

        @pl.when(more)
        def _():
            pack_s(s - 1)

        for c in range(CHUNKS):
            for k in range(1, experts):
                a_copy(c, k).wait()
            term = lax.dot_general(
                recv_a[:, cols(c)], wout[:, cols(c)], nt, preferred_element_type=jnp.float32
            )
            if c == 0:
                back[...] = term
            elif c < CHUNKS - 1:
                back[...] += term
            else:
                hidden[...] = ((back[...] + term) * slopes[...]).astype(jnp.bfloat16)
        for c in range(CHUNKS):
            send_b[:, cols(c)] = lax.dot_general(
                hidden[...], win[cols(c), :], nt, preferred_element_type=jnp.float32
            ).astype(jnp.bfloat16)
            for k in range(1, experts):
                b_copy(c, k).start()
            recv_b[own, cols(c)] = send_b[own, cols(c)]

        @pl.when(more)
        def _():
            make_slopes(s - 1)

        for c in range(CHUNKS):
            for k in range(1, experts):
                b_copy(c, k).wait()
            both = jnp.dot(cmat[s], recv_b[:, cols(c)], preferred_element_type=jnp.float32)
            adj[:, cols(c)] = adj[:, cols(c)] + (both[0:rows] + both[rows:])
            collect[s, :, cols(c)] = adj[:, cols(c)]

            @pl.when(more)
            def _():
                pack_a(s - 1, c)

        @pl.when(s == t)
        def _():
            out_local(s).start()

        @pl.when(s != t)
        def _():
            out_remote(s).start()

        return carry

    lax.fori_loop(0, steps, one_round, 0)

    out_local(t).wait()
    for k in range(1, steps):
        out_remote(tm_peer(k)).wait_send()
    for k in range(1, steps):
        b = tm_peer(k)
        remote(collect.at[b], out.at[0, block_rows(b)], o_ssem.at[b], o_rsem.at[b], "tm", b).wait_recv()


def per_device(states, terminal, gates, routes, w_in, w_out):
    steps = lax.axis_size("tm")
    experts = lax.axis_size("expert")
    width = states.shape[2]
    ff = w_in.shape[2]
    top = routes.shape[2]
    tokens = states.shape[1]
    rows = tokens // steps
    cap = min(rows, (3 * MB * top + 2 * experts - 1) // (2 * experts))
    slots = experts * PAD
    rg = jnp.concatenate([routes[0].astype(jnp.float32), gates[0]], axis=1)
    rg = jnp.pad(rg, ((0, 0), (0, 128 - 2 * top)))
    dma = pltpu.SemaphoreType.DMA
    bf = jnp.bfloat16
    return pl.pallas_call(
        functools.partial(kernel, steps, experts, cap, rows),
        out_shape=jax.ShapeDtypeStruct(states.shape, jnp.float32),
        in_specs=[pl.BlockSpec(memory_space=pl.ANY)] * 5,
        out_specs=pl.BlockSpec(memory_space=pl.ANY),
        scratch_shapes=[
            pltpu.VMEM((width, ff), bf),
            pltpu.VMEM((ff, width), bf),
            pltpu.VMEM((rows, width), jnp.float32),
            pltpu.VMEM((steps, rows, width), bf),
            pltpu.VMEM((steps, rows, 128), jnp.float32),
            pltpu.VMEM((steps, slots, rows), bf),
            pltpu.VMEM((steps, 2 * rows, slots), bf),
            pltpu.VMEM((steps, slots, width), bf),
            pltpu.VMEM((steps, slots, width), bf),
            pltpu.VMEM((slots, width), bf),
            pltpu.VMEM((slots, width), bf),
            pltpu.VMEM((slots, width), bf),
            pltpu.VMEM((slots, width), bf),
            pltpu.VMEM((slots, ff), jnp.float32),
            pltpu.VMEM((slots, ff), jnp.float32),
            pltpu.VMEM((slots, ff), bf),
            pltpu.VMEM((steps, rows, width), jnp.float32),
            dma((2, CHUNKS)),
            dma((4,)),
            dma((steps - 1,)),
            dma((steps - 1,)),
            dma((steps - 1,)),
            dma((steps - 1,)),
            dma((steps, experts - 1)),
            dma((steps, experts - 1)),
            dma((CHUNKS, experts - 1)),
            dma((CHUNKS, experts - 1)),
            dma((CHUNKS, experts - 1)),
            dma((CHUNKS, experts - 1)),
            dma((steps,)),
            dma((steps,)),
        ],
        compiler_params=pltpu.CompilerParams(
            collective_id=0, has_side_effects=True, vmem_limit_bytes=60 * 1024 * 1024
        ),
    )(states, terminal, rg, w_in, w_out)


def solution(mesh):
    placed = (
        P("tm", "expert", None),
        P("expert", None),
        P("tm", "expert", None),
        P("tm", "expert", None),
        P("expert", None, None),
        P("expert", None, None),
    )
    return jax.shard_map(
        per_device, mesh=mesh, in_specs=placed, out_specs=P("tm", "expert", None), check_vma=False
    )
```
